32 devices in a mesh: row: 2 (over x), col: 16 (over z, y, core).
Axes of the slice: x: 2, y: 2, z: 4, core: 2. Of those that a mesh axis runs over, the one named last changes fastest.
Arguments:
- trace_maps: bfloat16 [2, 16, 1280, 1280], P('row', 'col'), may hold values from -0.125 to 0.125
- sources: bfloat16 [2, 16, 1280, 256], P('row', 'col'), may hold values from -6 to 6
Outputs:
- traces: bfloat16 [2, 16, 1280, 256], P('row', 'col')
The draws below stay inside these ranges and needn't reach their ends.
All inputs are finite; a program needn't handle non-finite values.
Results may differ from the reference program's by a relative error of at most 0.007.
Values may be sent and summed in bfloat16 or wider, within the bound.
No kernel may reach another device: no remote copies, remote signals or barrier semaphores. Data moves between devices by JAX's collectives and lax.ppermute only.
A program may use at most 64 MiB of HBM per device.

```python
import jax
import jax.numpy as jnp
from jax import lax

TR = 640
RHS = 256
ITERS = 8
GR = 2
GC = 16


def shard_levels(key, extent, cuts, least, high):
    factor_of = 1.0
    for dim, shards_of in cuts:
        heights = jax.random.uniform(jax.random.fold_in(jax.random.fold_in(key, 6), dim), (shards_of,), jnp.float32, least / len(cuts), high / len(cuts))
        factor_of = factor_of * jnp.repeat(jnp.exp(heights), extent[dim] // shards_of).reshape((-1,) + (1,) * (len(extent) - 1 - dim))
    return factor_of


def gaussian(own_key, extent, scale, bound, pieces=(), dtype=jnp.bfloat16):
    values = jax.random.normal(own_key, extent, jnp.float32) * scale
    if len(pieces) > 0:
        values = shard_levels(own_key, extent, pieces, -0.22, 0.18) * values
    return jnp.clip(values, min=-bound, max=bound).astype(dtype)


def setup_inputs(seed: int = 0) -> dict:
    key_list = jax.random.split(jax.random.key(seed), 3)
    return {
        "trace_maps": gaussian(key_list[0], (GR, GC, 2 * TR, 2 * TR), (4 * TR) ** -0.5, 0.125, ((0, 2), (1, 16))),
        "sources": gaussian(key_list[1], (GR, GC, 2 * TR, RHS), 1.0, 6.0, ((0, 2), (1, 16))),
    }


def apply_maps(maps_flat, incoming_flat):
    def one_block(pair):
        return jnp.dot(pair[0], pair[1], preferred_element_type=jnp.float32)
    return lax.map(one_block, (maps_flat, incoming_flat))


def reference(trace_maps, sources):
    rows_grid, cols_grid, order, width = sources.shape
    half = order // 2
    source_float = sources.astype(jnp.float32)
    state = source_float
    maps_flat = trace_maps.reshape(rows_grid * cols_grid, order, order)
    for step in range(ITERS):
        sent = state.astype(jnp.bfloat16)
        right = sent[:, :, :half]
        upper = sent[:, :, half:]
        left_in = jnp.concatenate([jnp.zeros_like(right[:, :1]), right[:, :-1]], axis=1)
        below_in = jnp.concatenate([jnp.zeros_like(upper[:1]), upper[:-1]], axis=0)
        incoming = jnp.concatenate([left_in, below_in], axis=2)
        product = apply_maps(maps_flat, incoming.reshape(rows_grid * cols_grid, order, width))
        state = product.reshape(rows_grid, cols_grid, order, width) + source_float
    return state.astype(jnp.bfloat16)
```

```python
import functools

import jax
import jax.numpy as jnp
from jax import lax
from jax.experimental import pallas as pl
from jax.experimental.pallas import tpu as pltpu
from jax.sharding import PartitionSpec as P

ITERS = 8
LAG = 1

VMEM = pl.BlockSpec(memory_space=pltpu.VMEM)


def in_vmem(array):
    return pltpu.with_memory_space_constraint(array, pltpu.VMEM)


def call(body, name, outs, *operands):
    operands = [in_vmem(operand) for operand in operands]
    return pl.pallas_call(
        body,
        out_shape=[pltpu.VMEM(shape, jnp.bfloat16) for shape in outs],
        in_specs=[VMEM] * len(operands),
        out_specs=[VMEM] * len(outs),
        compiler_params=pltpu.CompilerParams(vmem_limit_bytes=12 * 1024 * 1024),
        cost_estimate=pl.CostEstimate(flops=1280 * 1280 * 256, bytes_accessed=4_000_000, transcendentals=0),
        name=name,
    )(*operands)


def dot(left, right):
    return jnp.dot(left, right, preferred_element_type=jnp.float32)


def split_body(source, kept, sent):
    width = kept.shape[1]
    core = lax.rem(lax.axis_index("col"), 2)
    for k in range(2):
        @pl.when(core == k)
        def _():
            kept[...] = source[:, k * width:(k + 1) * width]
            sent[...] = source[:, (1 - k) * width:(2 - k) * width]


def pick_body(column, rows, kept, got, right, upper):
    half = right.shape[0]
    core = lax.rem(lax.axis_index("col"), 2)
    for k in range(2):
        @pl.when(core == k)
        def _():
            ref = kept if k == column else got
            right[...] = ref[:half, :]
            upper[...] = ref[half:, :]


def step_body(column, slot, rows, map_own, map_got, right_in, upper_in, kept, got, old_right, old_upper, right, upper):
    half = right.shape[0]
    row = lax.axis_index("row")
    core = lax.rem(lax.axis_index("col"), 2)
    time = slot - LAG * row
    active = jnp.logical_and(time >= 0, time < ITERS - 1)
    for k in range(2):
        mapping, source = (map_own, kept) if k == column else (map_got, got)
        here = jnp.logical_and(active, core == k)

        @pl.when(jnp.logical_and(here, row == 0))
        def _():
            total = dot(mapping[:, :half], right_in[...]) + source[...].astype(jnp.float32)
            right[...] = total[:half].astype(right.dtype)
            upper[...] = total[half:].astype(upper.dtype)

        @pl.when(jnp.logical_and(here, jnp.logical_and(row > 0, row == rows - 1)))
        def _():
            total = dot(mapping[:half, :half], right_in[...]) + dot(mapping[:half, half:], upper_in[...])
            right[...] = (total + source[:half, :].astype(jnp.float32)).astype(right.dtype)
            upper[...] = old_upper[...]

        if rows > 2:
            @pl.when(jnp.logical_and(here, jnp.logical_and(row > 0, row < rows - 1)))
            def _():
                total = dot(mapping[:, :half], right_in[...]) + dot(mapping[:, half:], upper_in[...])
                total = total + source[...].astype(jnp.float32)
                right[...] = total[:half].astype(right.dtype)
                upper[...] = total[half:].astype(upper.dtype)

    @pl.when(jnp.logical_not(active))
    def _():
        right[...] = old_right[...]
        upper[...] = old_upper[...]


def give_body(first, second, sent):
    core = lax.rem(lax.axis_index("col"), 2)

    @pl.when(core == 0)
    def _():
        sent[...] = first[...]

    @pl.when(core == 1)
    def _():
        sent[...] = second[...]


def join_body(first, second, got, whole):
    width = got.shape[1]
    core = lax.rem(lax.axis_index("col"), 2)

    @pl.when(core == 0)
    def _():
        whole[:, :width] = first[...]
        whole[:, width:] = got[...]

    @pl.when(core == 1)
    def _():
        whole[:, :width] = got[...]
        whole[:, width:] = second[...]


def last_body(mapping, right_in, upper_in, source, out):
    half = right_in.shape[0]
    total = dot(mapping[:, :half], right_in[...]) + source[...].astype(jnp.float32)
    out[...] = (total + dot(mapping[:, half:], upper_in[...])).astype(out.dtype)


def per_device(trace_maps, sources):
    mapping = trace_maps[0, 0]
    source = sources[0, 0]
    order, width = source.shape
    half, part = order // 2, width // 2
    rows = lax.axis_size("row")
    count = lax.axis_size("col")
    swap = [(j, j ^ 1) for j in range(count)]
    cross = [(j, j + 2) for j in range(count - 2)]
    slots = ITERS - 1 + LAG * (rows - 1)
    last_message = ITERS - 2 + LAG * (rows - 2)

    def exchange(array):
        return lax.ppermute(array, "col", swap)

    def rightward(array):
        return lax.ppermute(array, "col", cross)

    def upward(array, slot):
        pairs = []
        for i in range(rows - 1):
            time = slot + 1 - LAG * i
            if 0 <= time and (time < ITERS or slot == last_message):
                pairs.append((i, i + 1))
        return lax.ppermute(array, "row", pairs)

    kept, sent = call(split_body, "split", [(order, part)] * 2, source)
    got = exchange(sent)
    map_got = exchange(mapping)
    trace = (half, part)
    pick = lambda column: call(functools.partial(pick_body, column, rows), f"pick{column}", [trace] * 2, kept, got)
    right_a, upper_a = pick(0)
    right_b, upper_b = pick(1)
    left = rightward(right_b)
    below_b, below_a = [upward(upper_b, -1)], [upward(upper_a, -1)]

    def advance(column, slot, right_in, upper_in, old_right, old_upper):
        body = functools.partial(step_body, column, slot, rows)
        return call(body, f"step{slot}_{column}", [trace] * 2, mapping, map_got, right_in, upper_in, kept, got, old_right, old_upper)

    zero = jnp.zeros(trace, jnp.bfloat16)
    for slot in range(slots):
        message = slot - 1 - LAG
        in_b = below_b[message + 1] if message >= -1 else zero
        in_a = below_a[message + 1] if message >= -1 else zero
        new_right_b, upper_b = advance(1, slot, right_a, in_b, right_b, upper_b)
        new_left = rightward(new_right_b)
        if slot < last_message:
            below_b.append(upward(upper_b, slot))
        right_a, upper_a = advance(0, slot, left, in_a, right_a, upper_a)
        if slot < last_message:
            below_a.append(upward(upper_a, slot))
        elif slot == last_message:
            given, = call(give_body, "give_upper", [trace], upper_b, upper_a)
            whole, = call(join_body, "join_upper", [(half, width)], upper_a, upper_b, exchange(given))
            below_last = upward(whole, slot)
        right_b, left = new_right_b, new_left

    given, = call(give_body, "give_right", [trace], right_a, left)
    right_in, = call(join_body, "join_right", [(half, width)], left, right_a, exchange(given))
    out, = call(last_body, "last", [(order, width)], mapping, right_in, below_last, source)
    return out[None, None]


def solution(mesh):
    placed = (P("row", "col", None, None), P("row", "col", None, None))
    return jax.shard_map(
        per_device,
        mesh=mesh,
        in_specs=placed,
        out_specs=P("row", "col", None, None),
        check_vma=False,
    )
```

```python
import functools

import jax
import jax.numpy as jnp
from jax import lax
from jax.experimental import pallas as pl
from jax.experimental.pallas import tpu as pltpu
from jax.sharding import PartitionSpec as P


ITERS = 8
LAG = 1

LIMIT = 12 * 1024 * 1024
COST = pl.CostEstimate(flops=400_000_000, bytes_accessed=2_000_000, transcendentals=0)
VMEM = pl.BlockSpec(memory_space=pltpu.VMEM)


def in_vmem(array):
    return pltpu.with_memory_space_constraint(array, pltpu.VMEM)


def call(body, outs, *operands):
    operands = [in_vmem(operand) for operand in operands]
    return pl.pallas_call(
        body,
        out_shape=[pltpu.VMEM(*(out if isinstance(out[0], tuple) else (out, jnp.bfloat16))) for out in outs],
        in_specs=[VMEM] * len(operands),
        out_specs=[VMEM] * len(outs),
        compiler_params=pltpu.CompilerParams(vmem_limit_bytes=LIMIT),
        cost_estimate=COST,
    )(*operands)


def dot(left, right):
    return jnp.dot(left, right, preferred_element_type=jnp.float32)


def pick_body(own, got, source_a, source_b, right_a, upper_a, right_b, upper_b):
    half, width = right_a.shape
    core = lax.rem(lax.axis_index("col"), 2)
    for k in range(2):
        @pl.when(core == k)
        def _():
            first, second = (own, got) if k == 0 else (got, own)
            part = slice(k * width, (k + 1) * width)
            source_a[...] = first[:, part]
            source_b[...] = second[:, part]
            right_a[...] = first[:half, part]
            upper_a[...] = first[half:, part]
            right_b[...] = second[:half, part]
            upper_b[...] = second[half:, part]


def sort_body(own, got, map_a, map_b):
    core = lax.rem(lax.axis_index("col"), 2)

    def copy(k, first, second):
        @pl.when(core == k)
        def _():
            @pl.loop(0, first.shape[0] // 128)
            def _(i):
                rows = pl.ds(pl.multiple_of(i * 128, 128), 128)
                map_a[rows, :] = first[rows, :]
                map_b[rows, :] = second[rows, :]

    copy(0, own, got)
    copy(1, got, own)


def step_body(slot, rows, mapping, right_in, upper_in, source, old_right, old_upper, right, upper):
    half = right.shape[0]
    row = lax.axis_index("row")
    time = slot - LAG * row
    active = jnp.logical_and(time >= 0, time < ITERS - 1)

    @pl.when(jnp.logical_and(active, row == 0))
    def _():
        total = dot(mapping[:, :half], right_in[...]) + source[...].astype(jnp.float32)
        right[...] = total[:half].astype(right.dtype)
        upper[...] = total[half:].astype(upper.dtype)

    @pl.when(jnp.logical_and(active, jnp.logical_and(row > 0, row == rows - 1)))
    def _():
        total = dot(mapping[:half, :half], right_in[...]) + dot(mapping[:half, half:], upper_in[...])
        right[...] = (total + source[:half, :].astype(jnp.float32)).astype(right.dtype)
        upper[...] = old_upper[...]

    if rows > 2:
        @pl.when(jnp.logical_and(active, jnp.logical_and(row > 0, row < rows - 1)))
        def _():
            total = dot(mapping[:, :half], right_in[...]) + dot(mapping[:, half:], upper_in[...])
            total = total + source[...].astype(jnp.float32)
            right[...] = total[:half].astype(right.dtype)
            upper[...] = total[half:].astype(upper.dtype)

    @pl.when(jnp.logical_not(active))
    def _():
        right[...] = old_right[...]
        upper[...] = old_upper[...]


def give_body(first, second, sent):
    core = lax.rem(lax.axis_index("col"), 2)

    @pl.when(core == 0)
    def _():
        sent[...] = first[...]

    @pl.when(core == 1)
    def _():
        sent[...] = second[...]


def join_body(first, second, got, whole):
    width = got.shape[1]
    core = lax.rem(lax.axis_index("col"), 2)

    @pl.when(core == 0)
    def _():
        whole[:, :width] = first[...]
        whole[:, width:] = got[...]

    @pl.when(core == 1)
    def _():
        whole[:, :width] = got[...]
        whole[:, width:] = second[...]


def begin_body(mapping, right_in, source, total):
    half = right_in.shape[0]
    total[...] = dot(mapping[:, :half], right_in[...]) + source[...].astype(jnp.float32)


def last_body(mapping, total, upper_in, out, ready, sems):
    half = upper_in.shape[0]
    parts = sems.shape[0]
    tall = total.shape[0] // parts
    copies = []
    for n in range(parts):
        rows = slice(n * tall, (n + 1) * tall)
        ready[rows, :] = (total[rows, :] + dot(mapping[rows, half:], upper_in[...])).astype(ready.dtype)
        copy = pltpu.make_async_copy(ready.at[rows, :], out.at[rows, :], sems.at[n])
        copy.start()
        copies.append(copy)
    for copy in copies:
        copy.wait()


def last(mapping, total, upper_in, shape):
    operands = [in_vmem(operand) for operand in (mapping, total, upper_in)]
    return pl.pallas_call(
        last_body,
        out_shape=jax.ShapeDtypeStruct(shape, jnp.bfloat16),
        in_specs=[VMEM] * 3,
        out_specs=pl.BlockSpec(memory_space=pltpu.HBM),
        scratch_shapes=[pltpu.VMEM(shape, jnp.bfloat16), pltpu.SemaphoreType.DMA((2,))],
        compiler_params=pltpu.CompilerParams(vmem_limit_bytes=LIMIT),
        cost_estimate=COST,
        name="last",
    )(*operands)


def relax(trace_maps, sources):
    mapping = trace_maps[0, 0]
    source = sources[0, 0]
    order, width = source.shape
    half, part = order // 2, width // 2
    rows = lax.axis_size("row")
    count = lax.axis_size("col")
    swap = [(j, j ^ 1) for j in range(count)]
    cross = [(j, j + 2) for j in range(count - 2)]
    slots = ITERS - 1 + LAG * (rows - 1)
    last_message = ITERS - 2 + LAG * (rows - 2)

    def exchange(array):
        return lax.ppermute(array, "col", swap)

    def rightward(array):
        return lax.ppermute(array, "col", cross)

    def upward(array, slot):
        pairs = []
        for i in range(rows - 1):
            time = slot + 1 - LAG * i
            if 0 <= time and (time < ITERS or slot == last_message):
                pairs.append((i, i + 1))
        return lax.ppermute(array, "row", pairs)

    source_got = exchange(source)
    map_got = exchange(mapping)
    trace, state = (half, part), (order, part)
    source_a, source_b, right_a, upper_a, right_b, upper_b = call(
        pick_body, [state] * 2 + [trace] * 4, source, source_got)
    below_b = [upward(upper_b, -1)]
    left = rightward(right_b)
    below_a = [upward(upper_a, -1)]
    map_a, map_b = call(sort_body, [(order, order)] * 2, mapping, map_got)

    def advance(slot, *operands):
        body = functools.partial(step_body, slot, rows)
        return call(body, [trace] * 2, *operands)

    zero = jnp.zeros(trace, jnp.bfloat16)
    for slot in range(slots):
        message = slot - 1 - LAG
        in_b = below_b[message + 1] if message >= -1 else zero
        in_a = below_a[message + 1] if message >= -1 else zero
        new_right_b, upper_b = advance(slot, map_b, right_a, in_b, source_b, right_b, upper_b)
        new_left = rightward(new_right_b)
        if slot < last_message:
            below_b.append(upward(upper_b, slot))
        right_a, upper_a = advance(slot, map_a, left, in_a, source_a, right_a, upper_a)
        if slot < last_message:
            below_a.append(upward(upper_a, slot))
        elif slot == last_message:
            given, = call(give_body, [trace], upper_b, upper_a)
            whole, = call(join_body, [(half, width)], upper_a, upper_b, exchange(given))
            below_last = upward(whole, slot)
        right_b, left = new_right_b, new_left

    given, = call(give_body, [trace], right_a, left)
    right_in, = call(join_body, [(half, width)], left, right_a, exchange(given))
    total, = call(begin_body, [((order, width), jnp.float32)], mapping, right_in, source)
    out = last(mapping, total, below_last, (order, width))
    return out[None, None]


def solution(mesh):
    placed = (P("row", "col", None, None), P("row", "col", None, None))
    return jax.shard_map(
        relax,
        mesh=mesh,
        in_specs=placed,
        out_specs=P("row", "col", None, None),
        check_vma=False,
    )
```

```python
import functools

import jax
import jax.numpy as jnp
from jax import lax
from jax.experimental import pallas as pl
from jax.experimental.pallas import tpu as pltpu
from jax.sharding import PartitionSpec as P


ITERS = 8
LAG = 1

LIMIT = 12 * 1024 * 1024
COST = pl.CostEstimate(flops=400_000_000, bytes_accessed=2_000_000, transcendentals=0)
VMEM = pl.BlockSpec(memory_space=pltpu.VMEM)


def in_vmem(array):
    return pltpu.with_memory_space_constraint(array, pltpu.VMEM)


def call(body, outs, *operands):
    operands = [in_vmem(operand) for operand in operands]
    return pl.pallas_call(
            body,
            out_shape=[pltpu.VMEM(*(out if isinstance(out[0], tuple) else (out, jnp.bfloat16))) for out in outs],
            in_specs=[VMEM] * len(operands),
            out_specs=[VMEM] * len(outs),
            compiler_params=pltpu.CompilerParams(vmem_limit_bytes=LIMIT),
            cost_estimate=COST,
    )(*operands)


def dot(left, right):
    return jnp.dot(left, right, preferred_element_type=jnp.float32)


def load_body(mapping, source, map_own, source_own, sems):
    copies = [
        pltpu.make_async_copy(source, source_own, sems.at[0]),
        pltpu.make_async_copy(mapping, map_own, sems.at[1]),
    ]
    for copy in copies:
        copy.start()
    for copy in copies:
        copy.wait()


def load(mapping, source):
    return pl.pallas_call(
        load_body,
        out_shape=[pltpu.VMEM(array.shape, array.dtype) for array in (mapping, source)],
        in_specs=[pl.BlockSpec(memory_space=pltpu.HBM)] * 2,
        out_specs=[VMEM] * 2,
        scratch_shapes=[pltpu.SemaphoreType.DMA((2,))],
        compiler_params=pltpu.CompilerParams(vmem_limit_bytes=LIMIT),
        cost_estimate=COST,
        name="load",
    )(*[pltpu.with_memory_space_constraint(array, pltpu.HBM) for array in (mapping, source)])


def pick_body(own, got, source_a, source_b, right_a, upper_a, right_b, upper_b):
    half, width = right_a.shape
    core = lax.rem(lax.axis_index("col"), 2)
    for k in range(2):
        @pl.when(core == k)
        def _():
            first, second = (own, got) if k == 0 else (got, own)
            part = slice(k * width, (k + 1) * width)
            source_a[...] = first[:, part]
            source_b[...] = second[:, part]
            right_a[...] = first[:half, part]
            upper_a[...] = first[half:, part]
            right_b[...] = second[:half, part]
            upper_b[...] = second[half:, part]


def sort_body(own, got, map_a, map_b):
    core = lax.rem(lax.axis_index("col"), 2)

    def copy(k, first, second):
        @pl.when(core == k)
        def _():
            @pl.loop(0, first.shape[0] // 128)
            def _(i):
                rows = pl.ds(pl.multiple_of(i * 128, 128), 128)
                map_a[rows, :] = first[rows, :]
                map_b[rows, :] = second[rows, :]

    copy(0, own, got)
    copy(1, got, own)


def incoming(first, right_in):
    if not first:
        return right_in[...]
    return jnp.where(lax.axis_index("col") < 2, jnp.zeros_like(right_in), right_in[...])


def step_body(first, slot, rows, mapping, right_in, upper_in, source, old_right, old_upper, right, upper):
    half = right.shape[0]
    row = lax.axis_index("row")
    time = slot - LAG * row
    active = jnp.logical_and(time >= 0, time < ITERS - 1)

    @pl.when(jnp.logical_and(active, row == 0))
    def _():
        total = dot(mapping[:, :half], incoming(first, right_in)) + source[...].astype(jnp.float32)
        right[...] = total[:half].astype(right.dtype)
        upper[...] = total[half:].astype(upper.dtype)

    @pl.when(jnp.logical_and(active, jnp.logical_and(row > 0, row == rows - 1)))
    def _():
        total = dot(mapping[:half, :half], incoming(first, right_in)) + dot(mapping[:half, half:], upper_in[...])
        right[...] = (total + source[:half, :].astype(jnp.float32)).astype(right.dtype)
        upper[...] = old_upper[...]

    if rows > 2:
        @pl.when(jnp.logical_and(active, jnp.logical_and(row > 0, row < rows - 1)))
        def _():
            total = dot(mapping[:, :half], incoming(first, right_in)) + dot(mapping[:, half:], upper_in[...])
            total = total + source[...].astype(jnp.float32)
            right[...] = total[:half].astype(right.dtype)
            upper[...] = total[half:].astype(upper.dtype)

    @pl.when(jnp.logical_not(active))
    def _():
        right[...] = old_right[...]
        upper[...] = old_upper[...]


def give_body(first, second, sent):
    core = lax.rem(lax.axis_index("col"), 2)

    @pl.when(core == 0)
    def _():
        sent[...] = first[...]

    @pl.when(core == 1)
    def _():
        sent[...] = second[...]


def join_body(first, second, got, whole):
    width = got.shape[1]
    core = lax.rem(lax.axis_index("col"), 2)

    @pl.when(core == 0)
    def _():
        whole[:, :width] = first[...]
        whole[:, width:] = got[...]

    @pl.when(core == 1)
    def _():
        whole[:, :width] = got[...]
        whole[:, width:] = second[...]


def begin_body(mapping, right_in, source, total):
    half = right_in.shape[0]
    left = jnp.where(lax.axis_index("col") == 0, jnp.zeros_like(right_in), right_in[...])
    total[...] = dot(mapping[:, :half], left) + source[...].astype(jnp.float32)


def last_body(mapping, total, upper_in, out, ready, sems):
    half = upper_in.shape[0]
    parts = sems.shape[0]
    tall = total.shape[0] // parts
    copies = []
    below = jnp.where(lax.axis_index("row") == 0, jnp.zeros_like(upper_in), upper_in[...])
    for n in range(parts):
        rows = slice(n * tall, (n + 1) * tall)
        ready[rows, :] = (total[rows, :] + dot(mapping[rows, half:], below)).astype(ready.dtype)
        copy = pltpu.make_async_copy(ready.at[rows, :], out.at[rows, :], sems.at[n])
        copy.start()
        copies.append(copy)
    for copy in copies:
        copy.wait()


def last(mapping, total, upper_in, shape):
    operands = [in_vmem(operand) for operand in (mapping, total, upper_in)]
    return pl.pallas_call(
        last_body,
        out_shape=jax.ShapeDtypeStruct(shape, jnp.bfloat16),
        in_specs=[VMEM] * 3,
        out_specs=pl.BlockSpec(memory_space=pltpu.HBM),
        scratch_shapes=[pltpu.VMEM(shape, jnp.bfloat16), pltpu.SemaphoreType.DMA((2,))],
        compiler_params=pltpu.CompilerParams(vmem_limit_bytes=LIMIT),
        cost_estimate=COST,
        name="last",
    )(*operands)


def relax(trace_maps, sources):
    mapping = trace_maps[0, 0]
    source = sources[0, 0]
    order, width = source.shape
    half, part = order // 2, width // 2
    rows = lax.axis_size("row")
    count = lax.axis_size("col")
    swap = [(j, j ^ 1) for j in range(count)]
    cross = [(j, (j + 2) % count) for j in range(count)]
    up = [(i, (i + 1) % rows) for i in range(rows)]
    slots = ITERS - 1 + LAG * (rows - 1)
    last_message = ITERS - 2 + LAG * (rows - 2)

    def exchange(array):
        return lax.ppermute(array, "col", swap)

    def rightward(array):
        return lax.ppermute(array, "col", cross)

    def upward(array):
        return lax.ppermute(array, "row", up)

    source_got = exchange(source)
    map_got = exchange(mapping)
    map_own, source_own = load(mapping, source)
    trace, state = (half, part), (order, part)
    source_a, source_b, right_a, upper_a, right_b, upper_b = call(
        pick_body, [state] * 2 + [trace] * 4, source_own, source_got)
    below_b = [upward(upper_b)]
    left = rightward(right_b)
    below_a = [upward(upper_a)]
    map_a, map_b = call(sort_body, [(order, order)] * 2, map_own, map_got)

    def advance(column, slot, *operands):
        body = functools.partial(step_body, column == "a", slot, rows)
        return call(body, [trace] * 2, *operands)

    zero = jnp.zeros(trace, jnp.bfloat16)
    for slot in range(slots):
        message = slot - 1 - LAG
        in_b = below_b[message + 1] if message >= -1 else zero
        in_a = below_a[message + 1] if message >= -1 else zero
        new_right_b, upper_b = advance("b", slot, map_b, right_a, in_b, source_b, right_b, upper_b)
        new_left = rightward(new_right_b)
        if slot < last_message:
            below_b.append(upward(upper_b))
        right_a, upper_a = advance("a", slot, map_a, left, in_a, source_a, right_a, upper_a)
        if slot < last_message:
            below_a.append(upward(upper_a))
        elif slot == last_message:
            given, = call(give_body, [trace], upper_b, upper_a)
            whole, = call(join_body, [(half, width)], upper_a, upper_b, exchange(given))
            below_last = upward(whole)
        right_b, left = new_right_b, new_left

    given, = call(give_body, [trace], right_a, left)
    right_in, = call(join_body, [(half, width)], left, right_a, exchange(given))
    total, = call(begin_body, [((order, width), jnp.float32)], map_own, right_in, source_own)
    out = last(map_own, total, below_last, (order, width))
    return out[None, None]


def solution(mesh):
    placed = (P("row", "col", None, None), P("row", "col", None, None))

    return jax.shard_map(
        relax,
        mesh=mesh,
        in_specs=placed,
        out_specs=P("row", "col", None, None),
        check_vma=False,
    )
```

```python
import functools

import jax
import jax.numpy as jnp
from jax import lax
from jax.experimental import pallas as pl
from jax.experimental.pallas import tpu as pltpu
from jax.sharding import PartitionSpec as P


ITERS = 8
LAG = 1

LIMIT = 12 * 1024 * 1024
COST = pl.CostEstimate(flops=400_000_000, bytes_accessed=2_000_000, transcendentals=0)
VMEM = pl.BlockSpec(memory_space=pltpu.VMEM)


def in_vmem(array):
    return pltpu.with_memory_space_constraint(array, pltpu.VMEM)


def call(body, outs, *operands):
    operands = [in_vmem(operand) for operand in operands]
    return pl.pallas_call(
            body,
            out_shape=[pltpu.VMEM(*(out if isinstance(out[0], tuple) else (out, jnp.bfloat16))) for out in outs],
            in_specs=[VMEM] * len(operands),
            out_specs=[VMEM] * len(outs),
            compiler_params=pltpu.CompilerParams(vmem_limit_bytes=LIMIT),
            cost_estimate=COST,
    )(*operands)


def dot(left, right):
    return jnp.dot(left, right, preferred_element_type=jnp.float32)


def fetch(body, outs, operand):
    return pl.pallas_call(
        body,
        out_shape=[pltpu.VMEM(shape, operand.dtype) for shape in outs],
        in_specs=[pl.BlockSpec(memory_space=pltpu.HBM)],
        out_specs=[VMEM] * len(outs),
        scratch_shapes=[pltpu.SemaphoreType.DMA((len(outs),))],
        compiler_params=pltpu.CompilerParams(vmem_limit_bytes=LIMIT),
        cost_estimate=COST,
    )(pltpu.with_memory_space_constraint(operand, pltpu.HBM))


def load_map_body(mapping, map_own, sems):
    copy = pltpu.make_async_copy(mapping, map_own, sems.at[0])
    copy.start()
    copy.wait()


def load_source_body(source, upper, source_own, sems):
    half = upper.shape[0]
    copies = [
        pltpu.make_async_copy(source.at[half:, :], upper, sems.at[0]),
        pltpu.make_async_copy(source, source_own, sems.at[1]),
    ]
    for copy in copies:
        copy.start()
    for copy in copies:
        copy.wait()


def halve_body(whole, kept, sent):
    width = kept.shape[1]
    core = lax.rem(lax.axis_index("col"), 2)
    for k in range(2):
        @pl.when(core == k)
        def _():
            kept[...] = whole[:, k * width:(k + 1) * width]
            sent[...] = whole[:, (1 - k) * width:(2 - k) * width]


def order_body(own, got, first, second):
    core = lax.rem(lax.axis_index("col"), 2)
    for k in range(2):
        @pl.when(core == k)
        def _():
            first[...] = own[...] if k == 0 else got[...]
            second[...] = got[...] if k == 0 else own[...]


def pick_body(own, got, source_a, source_b, right_a, upper_a, right_b, upper_b):
    half, width = right_a.shape
    core = lax.rem(lax.axis_index("col"), 2)
    for k in range(2):
        @pl.when(core == k)
        def _():
            first, second = (own, got) if k == 0 else (got, own)
            part = slice(k * width, (k + 1) * width)
            source_a[...] = first[:, part]
            source_b[...] = second[:, part]
            right_a[...] = first[:half, part]
            upper_a[...] = first[half:, part]
            right_b[...] = second[:half, part]
            upper_b[...] = second[half:, part]


def sort_body(own, got, map_a, map_b):
    core = lax.rem(lax.axis_index("col"), 2)

    def copy(k, first, second):
        @pl.when(core == k)
        def _():
            @pl.loop(0, first.shape[0] // 128)
            def _(i):
                rows = pl.ds(pl.multiple_of(i * 128, 128), 128)
                map_a[rows, :] = first[rows, :]
                map_b[rows, :] = second[rows, :]

    copy(0, own, got)
    copy(1, got, own)


def incoming(first, right_in):
    if not first:
        return right_in[...]
    return jnp.where(lax.axis_index("col") < 2, jnp.zeros_like(right_in), right_in[...])


def step_body(first, slot, rows, mapping, right_in, upper_in, source, old_right, old_upper, right, upper):
    half = right.shape[0]
    row = lax.axis_index("row")
    time = slot - LAG * row
    active = jnp.logical_and(time >= 0, time < ITERS - 1)

    @pl.when(jnp.logical_and(active, row == 0))
    def _():
        total = dot(mapping[:, :half], incoming(first, right_in)) + source[...].astype(jnp.float32)
        right[...] = total[:half].astype(right.dtype)
        upper[...] = total[half:].astype(upper.dtype)

    @pl.when(jnp.logical_and(active, jnp.logical_and(row > 0, row == rows - 1)))
    def _():
        total = dot(mapping[:half, :half], incoming(first, right_in)) + dot(mapping[:half, half:], upper_in[...])
        right[...] = (total + source[:half, :].astype(jnp.float32)).astype(right.dtype)
        upper[...] = old_upper[...]

    if rows > 2:
        @pl.when(jnp.logical_and(active, jnp.logical_and(row > 0, row < rows - 1)))
        def _():
            total = dot(mapping[:, :half], incoming(first, right_in)) + dot(mapping[:, half:], upper_in[...])
            total = total + source[...].astype(jnp.float32)
            right[...] = total[:half].astype(right.dtype)
            upper[...] = total[half:].astype(upper.dtype)

    @pl.when(jnp.logical_not(active))
    def _():
        right[...] = old_right[...]
        upper[...] = old_upper[...]


def give_body(first, second, sent):
    core = lax.rem(lax.axis_index("col"), 2)

    @pl.when(core == 0)
    def _():
        sent[...] = first[...]

    @pl.when(core == 1)
    def _():
        sent[...] = second[...]


def join_body(first, second, got, whole):
    width = got.shape[1]
    core = lax.rem(lax.axis_index("col"), 2)

    @pl.when(core == 0)
    def _():
        whole[:, :width] = first[...]
        whole[:, width:] = got[...]

    @pl.when(core == 1)
    def _():
        whole[:, :width] = got[...]
        whole[:, width:] = second[...]


def begin_body(mapping, upper_in, source, total):
    half = upper_in.shape[0]
    below = jnp.where(lax.axis_index("row") == 0, jnp.zeros_like(upper_in), upper_in[...])
    total[...] = dot(mapping[:, half:], below) + source[...].astype(jnp.float32)


def last_body(mapping, total, right_in, out, ready, sems):
    half = right_in.shape[0]
    parts = sems.shape[0]
    tall = total.shape[0] // parts
    copies = []
    left = jnp.where(lax.axis_index("col") == 0, jnp.zeros_like(right_in), right_in[...])
    for n in range(parts):
        rows = slice(n * tall, (n + 1) * tall)
        ready[rows, :] = (total[rows, :] + dot(mapping[rows, :half], left)).astype(ready.dtype)
        copy = pltpu.make_async_copy(ready.at[rows, :], out.at[rows, :], sems.at[n])
        copy.start()
        copies.append(copy)
    for copy in copies:
        copy.wait()


def last(mapping, total, right_in, shape):
    operands = [in_vmem(operand) for operand in (mapping, total, right_in)]
    return pl.pallas_call(
        last_body,
        out_shape=jax.ShapeDtypeStruct(shape, jnp.bfloat16),
        in_specs=[VMEM] * 3,
        out_specs=pl.BlockSpec(memory_space=pltpu.HBM),
        scratch_shapes=[pltpu.VMEM(shape, jnp.bfloat16), pltpu.SemaphoreType.DMA((4,))],
        compiler_params=pltpu.CompilerParams(vmem_limit_bytes=LIMIT),
        cost_estimate=COST,
        name="last",
    )(*operands)


def relax(trace_maps, sources):
    mapping = trace_maps[0, 0]
    source = sources[0, 0]
    order, width = source.shape
    half, part = order // 2, width // 2
    rows = lax.axis_size("row")
    count = lax.axis_size("col")
    swap = [(j, j ^ 1) for j in range(count)]
    cross = [(j, (j + 2) % count) for j in range(count)]
    up = [(i, (i + 1) % rows) for i in range(rows)]
    slots = ITERS - 1 + LAG * (rows - 1)
    last_message = ITERS - 2 + LAG * (rows - 2)

    def exchange(array):
        return lax.ppermute(array, "col", swap)

    def rightward(array, wrap=True):
        return lax.ppermute(array, "col", cross if wrap else cross[:-2])

    def upward(array):
        return lax.ppermute(array, "row", up)

    source_got = exchange(source)
    map_got = exchange(mapping)
    trace, state = (half, part), (order, part)
    upper_own, source_own = fetch(load_source_body, [(half, width), (order, width)], source)
    below_own = upward(upper_own)
    map_own, = fetch(load_map_body, [(order, order)], mapping)
    source_a, source_b, right_a, upper_a, right_b, upper_b = call(
        pick_body, [state] * 2 + [trace] * 4, source_own, source_got)
    left = rightward(right_b)
    map_a, map_b = call(sort_body, [(order, order)] * 2, map_own, map_got)

    def advance(column, slot, *operands):
        body = functools.partial(step_body, column == "a", slot, rows)
        return call(body, [trace] * 2, *operands)

    zero = jnp.zeros(trace, jnp.bfloat16)
    below_a, below_b = [None], [None]
    for slot in range(slots):
        message = slot - 1 - LAG
        if message == -1:
            kept, sent = call(halve_body, [trace] * 2, below_own)
            below_a[0], below_b[0] = call(order_body, [trace] * 2, kept, exchange(sent))
        in_b = below_b[message + 1] if message >= -1 else zero
        in_a = below_a[message + 1] if message >= -1 else zero
        new_right_b, upper_b = advance("b", slot, map_b, right_a, in_b, source_b, right_b, upper_b)
        new_left = rightward(new_right_b, wrap=slot < slots - 1)
        if slot < last_message:
            below_b.append(upward(upper_b))
        right_a, upper_a = advance("a", slot, map_a, left, in_a, source_a, right_a, upper_a)
        if slot < last_message:
            below_a.append(upward(upper_a))
        elif slot == last_message:
            given, = call(give_body, [trace], upper_b, upper_a)
            whole, = call(join_body, [(half, width)], upper_a, upper_b, exchange(given))
            below_last = upward(whole)
        right_b, left = new_right_b, new_left

    given, = call(give_body, [trace], right_a, left)
    got = exchange(given)
    total, = call(begin_body, [((order, width), jnp.float32)], map_own, below_last, source_own)
    right_in, = call(join_body, [(half, width)], left, right_a, got)
    out = last(map_own, total, right_in, (order, width))
    return out[None, None]


def solution(mesh):
    placed = (P("row", "col", None, None), P("row", "col", None, None))

    return jax.shard_map(
        relax,
        mesh=mesh,
        in_specs=placed,
        out_specs=P("row", "col", None, None),
        check_vma=False,
    )
```

```python
import functools

import jax
import jax.numpy as jnp
from jax import lax
from jax.experimental import pallas as pl
from jax.experimental.pallas import tpu as pltpu
from jax.sharding import PartitionSpec as P


ITERS = 8
LAG = 1

LIMIT = 12 * 1024 * 1024
COST = pl.CostEstimate(flops=400_000_000, bytes_accessed=2_000_000, transcendentals=0)
VMEM = pl.BlockSpec(memory_space=pltpu.VMEM)


def in_vmem(array):
    return pltpu.with_memory_space_constraint(array, pltpu.VMEM)


def call(body, outs, *operands):
    operands = [in_vmem(operand) for operand in operands]
    return pl.pallas_call(
            body,
            out_shape=[pltpu.VMEM(*(out if isinstance(out[0], tuple) else (out, jnp.bfloat16))) for out in outs],
            in_specs=[VMEM] * len(operands),
            out_specs=[VMEM] * len(outs),
            compiler_params=pltpu.CompilerParams(vmem_limit_bytes=LIMIT),
            cost_estimate=COST,
    )(*operands)


def dot(left, right):
    return jnp.dot(left, right, preferred_element_type=jnp.float32)


def fetch(body, outs, operand):
    return pl.pallas_call(
        body,
        out_shape=[pltpu.VMEM(shape, operand.dtype) for shape in outs],
        in_specs=[pl.BlockSpec(memory_space=pltpu.HBM)],
        out_specs=[VMEM] * len(outs),
        scratch_shapes=[pltpu.SemaphoreType.DMA((len(outs),))],
        compiler_params=pltpu.CompilerParams(vmem_limit_bytes=LIMIT),
        cost_estimate=COST,
    )(pltpu.with_memory_space_constraint(operand, pltpu.HBM))


def load_map_body(mapping, map_own, sems):
    copy = pltpu.make_async_copy(mapping, map_own, sems.at[0])
    copy.start()
    copy.wait()


def load_source_body(source, upper, source_own, sems):
    half = upper.shape[0]
    copies = [
        pltpu.make_async_copy(source.at[half:, :], upper, sems.at[0]),
        pltpu.make_async_copy(source, source_own, sems.at[1]),
    ]
    for copy in copies:
        copy.start()
    for copy in copies:
        copy.wait()


def halve_body(whole, kept, sent):
    width = kept.shape[1]
    core = lax.rem(lax.axis_index("col"), 2)
    for k in range(2):
        @pl.when(core == k)
        def _():
            kept[...] = whole[:, k * width:(k + 1) * width]
            sent[...] = whole[:, (1 - k) * width:(2 - k) * width]


def order_body(own, got, first, second):
    core = lax.rem(lax.axis_index("col"), 2)
    for k in range(2):
        @pl.when(core == k)
        def _():
            first[...] = own[...] if k == 0 else got[...]
            second[...] = got[...] if k == 0 else own[...]


def pick_body(own, got, source_a, source_b, right_a, upper_a, right_b, upper_b):
    half, width = right_a.shape
    core = lax.rem(lax.axis_index("col"), 2)
    for k in range(2):
        @pl.when(core == k)
        def _():
            first, second = (own, got) if k == 0 else (got, own)
            part = slice(k * width, (k + 1) * width)
            source_a[...] = first[:, part]
            source_b[...] = second[:, part]
            right_a[...] = first[:half, part]
            upper_a[...] = first[half:, part]
            right_b[...] = second[:half, part]
            upper_b[...] = second[half:, part]


def sort_body(own, got, map_a, map_b):
    core = lax.rem(lax.axis_index("col"), 2)

    def copy(k, first, second):
        @pl.when(core == k)
        def _():
            @pl.loop(0, first.shape[0] // 128)
            def _(i):
                rows = pl.ds(pl.multiple_of(i * 128, 128), 128)
                map_a[rows, :] = first[rows, :]
                map_b[rows, :] = second[rows, :]

    copy(0, own, got)
    copy(1, got, own)


def incoming(first, right_in):
    if not first:
        return right_in[...]
    return jnp.where(lax.axis_index("col") < 2, jnp.zeros_like(right_in), right_in[...])


def settled_chips(rows):
    return max(0, (ITERS - 2 - rows) // 2 + 1)


def choose_body(rows, left_old, left_new, right_a, left, given):
    chip = lax.axis_index("col") // 2
    core = lax.rem(lax.axis_index("col"), 2)
    settled = chip <= settled_chips(rows)
    left[...] = jnp.where(settled, left_old[...], left_new[...])

    @pl.when(core == 0)
    def _():
        given[...] = right_a[...]

    @pl.when(core == 1)
    def _():
        given[...] = left[...]


def step_body(first, slot, rows, mapping, right_in, upper_in, source, old_right, old_upper, right, upper=None):
    half = right.shape[0]
    row = lax.axis_index("row")
    time = slot - LAG * row
    active = jnp.logical_and(time >= 0, time < ITERS - 1)

    @pl.when(jnp.logical_and(active, row == 0))
    def _():
        if upper is None:
            total = dot(mapping[:half, :half], incoming(first, right_in)) + source[:half, :].astype(jnp.float32)
            right[...] = total.astype(right.dtype)
        else:
            total = dot(mapping[:, :half], incoming(first, right_in)) + source[...].astype(jnp.float32)
            right[...] = total[:half].astype(right.dtype)
            upper[...] = total[half:].astype(upper.dtype)

    @pl.when(jnp.logical_and(active, jnp.logical_and(row > 0, jnp.logical_or(row == rows - 1, upper is None))))
    def _():
        total = dot(mapping[:half, :half], incoming(first, right_in)) + dot(mapping[:half, half:], upper_in[...])
        right[...] = (total + source[:half, :].astype(jnp.float32)).astype(right.dtype)
        if upper is not None:
            upper[...] = old_upper[...]

    if rows > 2 and upper is not None:
        @pl.when(jnp.logical_and(active, jnp.logical_and(row > 0, row < rows - 1)))
        def _():
            total = dot(mapping[:, :half], incoming(first, right_in)) + dot(mapping[:, half:], upper_in[...])
            total = total + source[...].astype(jnp.float32)
            right[...] = total[:half].astype(right.dtype)
            upper[...] = total[half:].astype(upper.dtype)

    @pl.when(jnp.logical_not(active))
    def _():
        right[...] = old_right[...]
        if upper is not None:
            upper[...] = old_upper[...]


def give_body(first, second, sent):
    core = lax.rem(lax.axis_index("col"), 2)

    @pl.when(core == 0)
    def _():
        sent[...] = first[...]

    @pl.when(core == 1)
    def _():
        sent[...] = second[...]


def join_body(first, second, got, whole):
    width = got.shape[1]
    core = lax.rem(lax.axis_index("col"), 2)

    @pl.when(core == 0)
    def _():
        whole[:, :width] = first[...]
        whole[:, width:] = got[...]

    @pl.when(core == 1)
    def _():
        whole[:, :width] = got[...]
        whole[:, width:] = second[...]


def begin_body(mapping, right_in, source, total):
    half = right_in.shape[0]
    left = jnp.where(lax.axis_index("col") == 0, jnp.zeros_like(right_in), right_in[...])
    total[...] = dot(mapping[:, :half], left) + source[...].astype(jnp.float32)


def last_body(mapping, total, upper_in, out, ready, sems):
    half = upper_in.shape[0]
    parts = sems.shape[0]
    tall = total.shape[0] // parts
    copies = []
    below = jnp.where(lax.axis_index("row") == 0, jnp.zeros_like(upper_in), upper_in[...])
    for n in range(parts):
        rows = slice(n * tall, (n + 1) * tall)
        ready[rows, :] = (total[rows, :] + dot(mapping[rows, half:], below)).astype(ready.dtype)
        copy = pltpu.make_async_copy(ready.at[rows, :], out.at[rows, :], sems.at[n])
        copy.start()
        copies.append(copy)
    for copy in copies:
        copy.wait()


def last(mapping, total, upper_in, shape):
    operands = [in_vmem(operand) for operand in (mapping, total, upper_in)]
    return pl.pallas_call(
        last_body,
        out_shape=jax.ShapeDtypeStruct(shape, jnp.bfloat16),
        in_specs=[VMEM] * 3,
        out_specs=pl.BlockSpec(memory_space=pltpu.HBM),
        scratch_shapes=[pltpu.VMEM(shape, jnp.bfloat16), pltpu.SemaphoreType.DMA((4,))],
        compiler_params=pltpu.CompilerParams(vmem_limit_bytes=LIMIT),
        cost_estimate=COST,
        name="last",
    )(*operands)


def relax(trace_maps, sources):
    mapping = trace_maps[0, 0]
    source = sources[0, 0]
    order, width = source.shape
    half, part = order // 2, width // 2
    rows = lax.axis_size("row")
    count = lax.axis_size("col")
    swap = [(j, j ^ 1) for j in range(count)]
    cross = [(j, (j + 2) % count) for j in range(count)]
    settled = settled_chips(rows)
    groups = (range(2 * settled), range(2 * settled, count))
    settled_apart = [(j, group.start + (j + 2 - group.start) % len(group)) for group in groups for j in group]
    up = [(i, (i + 1) % rows) for i in range(rows)]
    slots = ITERS - 1 + LAG * (rows - 1)
    last_message = ITERS - 2 + LAG * (rows - 2)

    def exchange(array):
        return lax.ppermute(array, "col", swap)

    def rightward(array, wrap=True):
        return lax.ppermute(array, "col", cross if wrap else settled_apart)

    def upward(array):
        return lax.ppermute(array, "row", up)

    source_got = exchange(source)
    map_got = exchange(mapping)
    trace, state = (half, part), (order, part)
    upper_own, source_own = fetch(load_source_body, [(half, width), (order, width)], source)
    below_own = upward(upper_own)
    map_own, = fetch(load_map_body, [(order, order)], mapping)
    source_a, source_b, right_a, upper_a, right_b, upper_b = call(
        pick_body, [state] * 2 + [trace] * 4, source_own, source_got)
    left = rightward(right_b)
    map_a, map_b = call(sort_body, [(order, order)] * 2, map_own, map_got)

    def advance(column, slot, *operands):
        body = functools.partial(step_body, column == "a", slot, rows)
        outs = call(body, [trace] * (1 if slot == slots - 1 else 2), *operands)
        return outs if len(outs) == 2 else (outs[0], None)

    zero = jnp.zeros(trace, jnp.bfloat16)
    below_a, below_b = [None], [None]
    for slot in range(slots):
        message = slot - 1 - LAG
        if message == -1:
            kept, sent = call(halve_body, [trace] * 2, below_own)
            below_a[0], below_b[0] = call(order_body, [trace] * 2, kept, exchange(sent))
        in_b = below_b[message + 1] if message >= -1 else zero
        in_a = below_a[message + 1] if message >= -1 else zero
        new_right_b, upper_b = advance("b", slot, map_b, right_a, in_b, source_b, right_b, upper_b)
        new_left = rightward(new_right_b, wrap=slot < slots - 1)
        if slot < last_message:
            below_b.append(upward(upper_b))
        right_a, upper_a = advance("a", slot, map_a, left, in_a, source_a, right_a, upper_a)
        if slot < last_message:
            below_a.append(upward(upper_a))
        elif slot == last_message:
            given, = call(give_body, [trace], upper_b, upper_a)
            whole, = call(join_body, [(half, width)], upper_a, upper_b, exchange(given))
            below_last = upward(whole)
        right_b, left_old, left = new_right_b, left, new_left

    left, given = call(functools.partial(choose_body, rows), [trace] * 2, left_old, left, right_a)
    got = exchange(given)
    right_in, = call(join_body, [(half, width)], left, right_a, got)
    total, = call(begin_body, [((order, width), jnp.float32)], map_own, right_in, source_own)
    out = last(map_own, total, below_last, (order, width))
    return out[None, None]


def solution(mesh):
    placed = (P("row", "col", None, None), P("row", "col", None, None))

    return jax.shard_map(
        relax,
        mesh=mesh,
        in_specs=placed,
        out_specs=P("row", "col", None, None),
        check_vma=False,
    )
```
